32 devices in a mesh: col: 8 (over z, x), row: 4 (over y, core).
Axes of the slice: x: 2, y: 2, z: 4, core: 2. Of those that a mesh axis runs over, the one named last changes fastest.
Arguments:
- loads: float32 [4, 16, 2, 16, 128], P('row', 'col'), may hold values from -100 to 100
- stiffness: float32 [4, 32, 128], P('row', 'col'), may hold values from 0.5 to 2
- tile_info: int32 [4, 32, 4], P('row', 'col'), may hold values from 0 to 15, as said below
- offsets: int32 [4, 32, 2, 128], P('row', 'col'), may hold values from 0 to 127
Outputs:
- forces: float32 [4, 32, 16, 128], P('row', 'col')
- residual: float32 [4, 16, 2, 16, 128], P('row', 'col')
The draws below stay inside these ranges and needn't reach their ends.
Inputs may be any that keep to these rules, and one draw needn't show every extreme that they name: tile_info[s, t] = (first block, second block, flag, direction): every contact of the tile has its first disk in block tile_info[s, t, 0] of slab s and its second in block tile_info[s, t, 1] of slab s + tile_info[s, t, 2], cyclically over 4 slabs. The flag is 0 or 1, the direction 0 to 5, the two blocks differ, and in each slab every block is the first block of exactly 2 tiles.
All inputs are finite; a program needn't handle non-finite values.
Results may differ from the reference program's by a relative error of at most 0.00012.
Values sent between devices are 32-bit elements; how exact they have to be, the bound alone decides.
A program may use at most 64 MiB of HBM per device.

```python
import math
import jax
import jax.numpy as jnp

TILE = 128
LOADS = 16
ITERS = 2
SLABS = 4
SBLK = 16
STILE = 32


def draw_loads(key, part):
    key_noise, key_disk, key_case = jax.random.split(key, 3)
    shape = (SLABS, SBLK, 2, LOADS, TILE)
    disk_power = jax.random.uniform(key_disk, (SLABS, SBLK, 1, 1, TILE))
    case_power = jax.random.uniform(key_case, (1, 1, 1, LOADS, 1))
    block_pos = jnp.arange(SBLK, dtype=jnp.float32)[None, :, None, None, None]
    slab_pos = jnp.arange(SLABS, dtype=jnp.float32)[:, None, None, None, None]
    position = (block_pos * SLABS + slab_pos) / (SBLK * SLABS)
    scaling = jnp.exp(2.302585 * (disk_power + case_power)) / 12.0
    noise = jnp.clip(jax.random.normal(key_noise, shape), -4.0, 4.0)
    growth = 1.0 + 2.0 * position
    return (noise * scaling * growth).astype(jnp.float32)


def draw_tile_info(key, part):
    key_order, key_second, key_upper, key_turn = jax.random.split(key, 4)
    orders = jax.vmap(lambda slab_key: jax.random.permutation(slab_key, STILE))(jax.random.split(key_order, SLABS))
    first_block = (orders % SBLK).astype(jnp.int32)
    step_ahead = jax.random.randint(key_second, (SLABS, STILE), 1, SBLK)
    second_block = ((first_block + step_ahead) % SBLK).astype(jnp.int32)
    upper_flag = (jax.random.randint(key_upper, (SLABS, STILE), 0, 4) == 0).astype(jnp.int32)
    direction = jax.random.randint(key_turn, (SLABS, STILE), 0, 6).astype(jnp.int32)
    return jnp.stack([first_block, second_block, upper_flag, direction], axis=2).astype(jnp.int32)


def place_ends(drawn, stream_key, smallest, largest):
    longest = drawn.shape.index(max(drawn.shape))
    spots = []
    for shift in (0, 1):
        where = [jax.random.randint(jax.random.fold_in(stream_key, axis), (), 0, length) for axis, length in enumerate(drawn.shape)]
        where[longest] = (where[longest] + shift) % drawn.shape[longest]
        spots.append(tuple(where))
    return drawn.at[spots[0]].set(smallest).at[spots[1]].set(largest)


def block_levels(rng, dims, pieces, smallest, high):
    def one(dim, parts):
        heights = jax.random.uniform(jax.random.fold_in(jax.random.fold_in(rng, 6), dim), (parts,), jnp.float32, smallest / len(pieces), high / len(pieces))
        return jnp.repeat(jnp.exp(heights), dims[dim] // parts).reshape((-1,) + (1,) * (len(dims) - dim - 1))

    loudness = one(*pieces[0])
    for cut in pieces[1:]:
        loudness = loudness * one(*cut)
    return loudness


def setup_inputs(seed: int = 0) -> dict:
    splits = jax.random.split(jax.random.key(seed), 5)
    return {
        "loads": draw_loads(jax.random.fold_in(splits[4], 71), 0),
        "stiffness": jnp.clip(jnp.exp(math.log(2.0) - 1.3862944 * jax.random.uniform(splits[1], (SLABS, STILE, TILE), jnp.float32) ** block_levels(splits[1], (SLABS, STILE, TILE), ((0, 4), (1, 8)), -0.2, 0.2)), 0.5, 2.0),
        "tile_info": draw_tile_info(jax.random.fold_in(splits[4], 71), 0),
        "offsets": place_ends(jax.random.randint(splits[3], (SLABS, STILE, 2, TILE), 0, TILE), jax.random.fold_in(splits[3], 1), 0, TILE - 1).astype(jnp.int32),
    }


ANGLE_STEP = math.pi / 6.0
EPS = 1e-6


def contact_normals(tile_info):
    angles = tile_info[:, :, 3].astype(jnp.float32) * ANGLE_STEP
    return jnp.stack([jnp.cos(angles), jnp.sin(angles)], axis=2)


def pick_blocks(disk_field, block_ids):
    return jax.vmap(lambda slab_rows, chosen: slab_rows[chosen])(disk_field, block_ids)


def pick_lanes(blocks, lane_ids):
    lane_index = jnp.broadcast_to(lane_ids[:, :, None, None, :], blocks.shape)
    return jnp.take_along_axis(blocks, lane_index, axis=4)


def transpose_apply(disk_field, stiffness, tile_info, offsets, normal):
    above_rows = jnp.roll(disk_field, -1, axis=0)
    first_rows = pick_lanes(pick_blocks(disk_field, tile_info[:, :, 0]), offsets[:, :, 0])
    second_same = pick_lanes(pick_blocks(disk_field, tile_info[:, :, 1]), offsets[:, :, 1])
    second_above = pick_lanes(pick_blocks(above_rows, tile_info[:, :, 1]), offsets[:, :, 1])
    second_rows = jnp.where(tile_info[:, :, 2][:, :, None, None, None] == 1, second_above, second_same)
    difference = first_rows - second_rows
    projected = normal[:, :, 0, None, None] * difference[:, :, 0] + normal[:, :, 1, None, None] * difference[:, :, 1]
    return stiffness[:, :, None, :] * projected


def assemble(forces, stiffness, tile_info, offsets, normal):
    slab_count = tile_info.shape[0]
    weighted = stiffness[:, :, None, :] * forces
    values = normal[:, :, :, None, None] * weighted[:, :, None]
    slab_index = jnp.arange(slab_count, dtype=jnp.int32)[:, None, None]
    first_index = (slab_index * SBLK + tile_info[:, :, 0][:, :, None]) * TILE + offsets[:, :, 0]
    upper_slab = (slab_index + tile_info[:, :, 2][:, :, None]) % slab_count
    second_index = (upper_slab * SBLK + tile_info[:, :, 1][:, :, None]) * TILE + offsets[:, :, 1]
    flattened = jnp.transpose(values, (0, 1, 4, 2, 3)).reshape(-1, 2, LOADS)
    totals = jnp.zeros((slab_count * SBLK * TILE, 2, LOADS), jnp.float32)
    totals = totals.at[first_index.reshape(-1)].add(flattened)
    totals = totals.at[second_index.reshape(-1)].add(-flattened)
    return jnp.transpose(totals.reshape(slab_count, SBLK, TILE, 2, LOADS), (0, 1, 3, 4, 2))


def reference(loads, stiffness, tile_info, offsets):
    normal = contact_normals(tile_info)
    residual = loads
    search = transpose_apply(residual, stiffness, tile_info, offsets, normal)
    forces = jnp.zeros_like(search)
    direction = search
    force_sq = jnp.sum(search * search, axis=(0, 1, 3))
    for iteration in range(ITERS):
        image_field = assemble(direction, stiffness, tile_info, offsets, normal)
        image_sq = jnp.sum(image_field * image_field, axis=(0, 1, 2, 4))
        step_size = force_sq / (image_sq + EPS)
        forces = forces + step_size[:, None] * direction
        residual = residual - step_size[:, None] * image_field
        if iteration + 1 < ITERS:
            search = transpose_apply(residual, stiffness, tile_info, offsets, normal)
            force_next = jnp.sum(search * search, axis=(0, 1, 3))
            direction = search + (force_next / (force_sq + EPS))[:, None] * direction
            force_sq = force_next
    return forces, residual
```

```python
import functools
import math

import jax
import jax.numpy as jnp
import numpy as np
from jax import lax
from jax.experimental import pallas as pl
from jax.experimental.pallas import tpu as pltpu
from jax.sharding import PartitionSpec as P

ITERS = 2


ANGLE_STEP = math.pi / 6.0
EPS = 1e-06


def shifted(block, axis, distance):
    devices = range(lax.axis_size(axis))
    route = [((i - distance) % len(devices), i) for i in devices]
    return lax.ppermute(block, axis, route)


def lane_tables(lane_ids):
    lane_index = jnp.arange(lane_ids.shape[-1], dtype=jnp.int32)
    return (lane_index[None, None, :, None] == lane_ids[:, :, None, :]).astype(jnp.float32)


def tile_normals(listing):
    angles = listing[:, 3].astype(jnp.float32) * ANGLE_STEP
    return jnp.stack([jnp.cos(angles), jnp.sin(angles)], axis=1)


def select(block_rows, lane_table):
    return jnp.einsum("xclk,xkm->xclm", block_rows, lane_table, precision=lax.Precision.HIGHEST)


def spread(values, lane_table):
    return jnp.einsum("xclm,xkm->xclk", values, lane_table, precision=lax.Precision.HIGHEST)


def contributions(weighted, normal, tables):
    values = normal[:, :, None, None] * weighted[:, None]
    return (spread(values, tables[:, 0]), spread(values, tables[:, 1]))


def deposit(first_part, second_part, first_ids, second_ids, side_ids, row_begin, row_count):
    pos_first = jnp.where(
        (first_ids >= row_begin) & (first_ids < row_begin + row_count), first_ids, row_count
    )
    pos_second = jnp.where(
        (second_ids >= row_begin) & (second_ids < row_begin + row_count), second_ids, row_count
    )
    buffer = jnp.zeros((row_count, 2) + first_part.shape[1:], jnp.float32)
    buffer = buffer.at[pos_first, 0].add(first_part, mode="drop")
    return buffer.at[pos_second, side_ids].add(-second_part, mode="drop")


def force_squares(values):
    return jnp.sum(values * values, axis=(0, 1, 3))


def image_squares(values):
    return jnp.sum(values * values, axis=(0, 1, 2, 4))


def local(loads, stiffness, tile_info, offsets):
    listing = tile_info[0]
    first_block = listing[:, 0]
    second_block = listing[:, 1]
    upper_flag = listing[:, 2]
    normal = tile_normals(listing)
    tables = lane_tables(offsets[0])
    spring = stiffness[0]
    block_count = loads.shape[1]

    def transpose_apply(disk_field):
        above_rows = shifted(disk_field, "row", -1)
        own_slab, upper_slab = (
            lax.all_gather(disk_field, "col", axis=1, tiled=True),
            lax.all_gather(above_rows, "col", axis=1, tiled=True),
        )
        own_slab = own_slab[0]
        upper_slab = upper_slab[0]
        first_rows = own_slab[first_block]
        second_rows = jnp.where(
            upper_flag[:, None, None, None] == 1, upper_slab[second_block], own_slab[second_block]
        )
        difference = select(first_rows, tables[:, 0]) - select(second_rows, tables[:, 1])
        projected = (
            normal[:, 0, None, None] * difference[:, 0]
            + normal[:, 1, None, None] * difference[:, 1]
        )
        return (spring[:, None, :] * projected)[None]

    def force_total(values):
        return lax.psum(force_squares(values), ("col", "row"))

    residual = loads
    search = transpose_apply(residual)
    forces = jnp.zeros_like(search)
    direction = search
    force_sq = force_total(search)
    for iteration in range(ITERS):
        weighted = spring[:, None, :] * direction[0]
        first_part, second_part = contributions(weighted, normal, tables)
        summed = lax.psum_scatter(
            deposit(
                first_part,
                second_part,
                first_block,
                second_block,
                upper_flag,
                jnp.int32(0),
                block_count * lax.axis_size("col"),
            ),
            "col",
            scatter_dimension=0,
            tiled=True,
        )
        lifted = shifted(summed[:, 1], "row", 1)
        image_field = (summed[:, 0] + lifted)[None]
        image_sq = lax.psum(image_squares(image_field), ("col", "row"))
        step_size = force_sq / (image_sq + EPS)
        forces = forces + step_size[:, None] * direction
        residual = residual - step_size[:, None] * image_field
        if iteration + 1 < ITERS:
            search = transpose_apply(residual)
            force_next = force_total(search)
            direction = search + (force_next / (force_sq + EPS))[:, None] * direction
            force_sq = force_next
    return (forces, residual)


MESH = pl.DeviceIdType.MESH
CORES = 2
SIDE = 2
UNROLL_CHUNKS = 2
REPLICATED_LIMIT = 8 * 1024 * 1024
COSINES = [float(v) for v in np.cos(np.arange(6, dtype=np.float32) * np.float32(ANGLE_STEP))]
SINES = [float(v) for v in np.sin(np.arange(6, dtype=np.float32) * np.float32(ANGLE_STEP))]


def gather_kernel(line, cols, x_ref, out_ref, send_sem, recv_sem, local_sem):
    col, row = lax.axis_index("col"), lax.axis_index("row")
    z, x = col // SIDE, lax.rem(col, SIDE)
    y, c = row // CORES, lax.rem(row, CORES)
    xa, ya = x + (1 - c) * (1 - 2 * x), y + c * (1 - 2 * y)
    xb, yb = x + c * (1 - 2 * x), y + (1 - c) * (1 - 2 * y)

    def device(zz, xx, yy, cc):
        return {"col": zz * SIDE + xx, "row": yy * CORES + cc}

    def chunk(zz, xx, yy, cc):
        return (yy * CORES + cc) * cols + zz * SIDE + xx

    along = [lax.rem(z + step, line) for step in range(line)]
    partner_a, partner_b = device(z, xa, ya, c), device(z, xb, yb, c)
    partner_core = device(z, x, y, 1 - c)

    barrier = pltpu.get_barrier_semaphore()
    peers = [device(zz, x, y, c) for zz in along[1:]] + [partner_a, partner_b, partner_core]
    for peer in peers:
        pl.semaphore_signal(barrier, inc=1, device_id=peer, device_id_type=MESH)
    me = chunk(z, x, y, c)
    keep = pltpu.make_async_copy(x_ref, out_ref.at[me], local_sem)
    keep.start()
    pl.semaphore_wait(barrier, len(peers))

    sent = []

    def send(index, peer, own=False):
        copy = pltpu.make_async_remote_copy(
            src_ref=x_ref if own else out_ref.at[index],
            dst_ref=out_ref.at[index],
            send_sem=send_sem.at[len(sent)],
            recv_sem=recv_sem.at[index],
            device_id=peer,
            device_id_type=MESH,
        )
        copy.start()
        sent.append(copy)

    def arrive(index):
        pltpu.make_async_remote_copy(
            src_ref=x_ref,
            dst_ref=out_ref.at[index],
            send_sem=send_sem.at[0],
            recv_sem=recv_sem.at[index],
            device_id=partner_core,
            device_id_type=MESH,
        ).wait_recv()

    for zz in along[1:]:
        send(me, device(zz, x, y, c), own=True)
    for peer in (partner_a, partner_b, partner_core):
        send(me, peer, own=True)
    order = [along[0]] + [along[s] for s in (1, line - 1)] + [along[s] for s in range(2, line - 1)]
    for position, zz in enumerate(order):
        if position:
            index = chunk(zz, x, y, c)
            arrive(index)
            for peer in (partner_a, partner_b, partner_core):
                send(index, peer)
    for zz in order:
        index = chunk(zz, xa, ya, c)
        arrive(index)
        send(index, partner_b)
        send(index, partner_core)
    for zz in order:
        index = chunk(zz, xb, yb, c)
        arrive(index)
        send(index, partner_core)
    for zz in order:
        index = chunk(zz, 1 - x, 1 - y, c)
        arrive(index)
        send(index, partner_core)
    for xx, yy in ((x, y), (xa, ya), (xb, yb), (1 - x, 1 - y)):
        for zz in order:
            arrive(chunk(zz, xx, yy, 1 - c))
    for copy in sent:
        copy.wait_send()
    keep.wait()


def solve_kernel(
    dims, info_ref, place_ref, all_ref, forces_ref, left_ref,
    search_a, search_b, image_a, image_b, rest_ref, cos_ref, sin_ref,
):
    slabs, blocks, per_blocks, per_tiles, cases, lanes = dims
    chunks = all_ref.shape[0]
    disk_rows = 2 * cases
    cols = chunks // slabs
    base = per_blocks * disk_rows
    for k in range(6):
        cos_ref[k] = COSINES[k]
        sin_ref[k] = SINES[k]

    def apply_both(read_block, search_ref, image_ref):
        image_ref[...] = jnp.zeros_like(image_ref)
        sub = lax.broadcasted_iota(jnp.int32, (lanes, lanes), 0)

        def body(step, total):
            parts = []
            for u in range(UNROLL_CHUNKS):
                piece = step * UNROLL_CHUNKS + u
                slab = piece // cols
                for k in range(per_tiles):
                    tile = piece * per_tiles + k
                    first = slab * blocks + info_ref[tile * 4]
                    upper = lax.rem(slab + info_ref[tile * 4 + 2], slabs)
                    second = upper * blocks + info_ref[tile * 4 + 1]
                    turn = info_ref[tile * 4 + 3]
                    n0, n1 = cos_ref[turn], sin_ref[turn]
                    spring = all_ref[piece, base + k : base + k + 1, :]
                    at = base + per_tiles + 2 * k
                    lane_i = all_ref[piece, at : at + 1, :].astype(jnp.int32)
                    lane_j = all_ref[piece, at + 1 : at + 2, :].astype(jnp.int32)
                    vi, vj = read_block(first), read_block(second)
                    pi = n0 * vi[:cases] + n1 * vi[cases:]
                    pj = n0 * vj[:cases] + n1 * vj[cases:]
                    gi = jnp.take_along_axis(
                        pi, jnp.broadcast_to(lane_i, pi.shape), axis=1, mode="promise_in_bounds"
                    )
                    gj = jnp.take_along_axis(
                        pj, jnp.broadcast_to(lane_j, pj.shape), axis=1, mode="promise_in_bounds"
                    )
                    value = spring * (gi - gj)
                    search_ref[tile] = value
                    total = total + value * value
                    weighted = spring * value
                    high = weighted.astype(jnp.bfloat16)
                    rest = weighted - high.astype(jnp.float32)
                    middle = rest.astype(jnp.bfloat16)
                    low = (rest - middle.astype(jnp.float32)).astype(jnp.bfloat16)
                    lhs = jnp.concatenate([high, middle, low], axis=0)
                    hot = jnp.concatenate(
                        [
                            jnp.where(sub == lane_i, 1.0, 0.0).astype(jnp.bfloat16),
                            jnp.where(sub == lane_j, 1.0, 0.0).astype(jnp.bfloat16),
                        ],
                        axis=0,
                    )
                    out = lax.dot_general(
                        lhs, hot, (((1,), (1,)), ((), ())), preferred_element_type=jnp.float32
                    )
                    out = out[:cases] + (out[cases : 2 * cases] + out[2 * cases :])
                    parts.append((first, second, n0, n1, out[:, :lanes], out[:, lanes:]))
            for first, second, n0, n1, one, two in parts:
                image_ref[first, :cases] += n0 * one
                image_ref[first, cases:] += n1 * one
                image_ref[second, :cases] -= n0 * two
                image_ref[second, cases:] -= n1 * two
            return total

        total = lax.fori_loop(
            0, chunks // UNROLL_CHUNKS, body, jnp.zeros((cases, lanes), jnp.float32)
        )
        return jnp.sum(total, axis=1, keepdims=True)

    def chunk_rows(block):
        start = pl.multiple_of(lax.rem(block, per_blocks) * disk_rows, 8)
        return all_ref[block // per_blocks, pl.ds(start, disk_rows), :]

    def squares(field):
        both = jnp.sum(field * field, axis=0)
        return both[:cases] + both[cases:]

    def over_chunks(visit):
        return jnp.sum(
            lax.fori_loop(
                0, chunks, visit, jnp.zeros((cases, lanes), jnp.float32), unroll=2
            ),
            axis=1,
            keepdims=True,
        )

    gamma = apply_both(chunk_rows, search_a, image_a)

    def norm_first(piece, total):
        return total + squares(image_a[pl.ds(piece * per_blocks, per_blocks)])

    alpha = gamma / (over_chunks(norm_first) + EPS)
    alpha_rows = jnp.concatenate([alpha, alpha], axis=0)

    def renew(piece, carry):
        for b in range(per_blocks):
            block = piece * per_blocks + b
            rest_ref[block] = (
                all_ref[piece, b * disk_rows : (b + 1) * disk_rows, :]
                - alpha_rows * image_a[block]
            )
        return carry

    lax.fori_loop(0, chunks, renew, 0, unroll=2)
    gamma_next = apply_both(lambda block: rest_ref[block], search_b, image_b)
    beta = gamma_next / (gamma + EPS)
    beta_rows = jnp.concatenate([beta, beta], axis=0)

    def norm_second(piece, total):
        span = pl.ds(piece * per_blocks, per_blocks)
        return total + squares(image_b[span] + beta_rows * image_a[span])

    alpha_next = gamma_next / (over_chunks(norm_second) + EPS)
    alpha_next_rows = jnp.concatenate([alpha_next, alpha_next], axis=0)
    place = place_ref[0]
    for k in range(per_tiles):
        tile = place * per_tiles + k
        old = search_a[tile]
        forces_ref[0, k] = alpha * old + alpha_next * (search_b[tile] + beta * old)
    for b in range(per_blocks):
        block = place * per_blocks + b
        left = rest_ref[block] - alpha_next_rows * (image_b[block] + beta_rows * image_a[block])
        left_ref[0, b, 0] = left[:cases]
        left_ref[0, b, 1] = left[cases:]


def replicated(cols, rows, loads, stiffness, tile_info, offsets):
    per_blocks, cases, lanes = loads.shape[1], loads.shape[3], loads.shape[4]
    per_tiles = stiffness.shape[1]
    chunks = cols * rows
    parts = [
        loads.reshape(-1, lanes),
        stiffness[0],
        offsets.reshape(-1, lanes).astype(jnp.float32),
        jnp.pad(tile_info[0].astype(jnp.float32), ((0, 0), (0, lanes - tile_info.shape[2]))),
    ]
    packed = jnp.concatenate(parts, axis=0)
    height = packed.shape[0]
    vmem = pl.BlockSpec(memory_space=pltpu.VMEM)
    smem = pl.BlockSpec(memory_space=pltpu.SMEM)
    everything = pl.pallas_call(
        functools.partial(gather_kernel, cols // SIDE, cols),
        out_shape=jax.ShapeDtypeStruct((chunks, height, lanes), jnp.float32),
        in_specs=[vmem],
        out_specs=vmem,
        scratch_shapes=[
            pltpu.SemaphoreType.DMA((chunks,)),
            pltpu.SemaphoreType.DMA((chunks,)),
            pltpu.SemaphoreType.DMA,
        ],
        compiler_params=pltpu.CompilerParams(collective_id=0, has_side_effects=True),
    )(packed)
    info = everything[:, height - per_tiles :, :4].astype(jnp.int32).reshape(-1)
    place = (lax.axis_index("row") * cols + lax.axis_index("col")).astype(jnp.int32)
    disk = (chunks * per_blocks, 2 * cases, lanes)
    contact = (chunks * per_tiles, cases, lanes)
    dims = (rows, cols * per_blocks, per_blocks, per_tiles, cases, lanes)
    return pl.pallas_call(
        functools.partial(solve_kernel, dims),
        out_shape=(
            jax.ShapeDtypeStruct((1, per_tiles, cases, lanes), jnp.float32),
            jax.ShapeDtypeStruct(loads.shape, jnp.float32),
        ),
        in_specs=[smem, smem, vmem],
        out_specs=(vmem, vmem),
        scratch_shapes=[
            pltpu.VMEM(contact, jnp.float32),
            pltpu.VMEM(contact, jnp.float32),
            pltpu.VMEM(disk, jnp.float32),
            pltpu.VMEM(disk, jnp.float32),
            pltpu.VMEM(disk, jnp.float32),
            pltpu.SMEM((6,), jnp.float32),
            pltpu.SMEM((6,), jnp.float32),
        ],
        compiler_params=pltpu.CompilerParams(vmem_limit_bytes=32 * 1024 * 1024),
    )(info, place[None], everything)


def program_body(cols, rows, loads, stiffness, tile_info, offsets):
    whole = cols * rows * loads.size * 4
    if whole <= REPLICATED_LIMIT and cols % SIDE == 0 and rows == SIDE * CORES:
        return replicated(cols, rows, loads, stiffness, tile_info, offsets)
    return local(loads, stiffness, tile_info, offsets)


def solution(mesh):
    placed = (
        P("row", "col", None, None, None),
        P("row", "col", None),
        P("row", "col", None),
        P("row", "col", None, None),
    )
    return jax.shard_map(
        functools.partial(program_body, mesh.shape["col"], mesh.shape["row"]),
        mesh=mesh,
        in_specs=placed,
        out_specs=(P("row", "col", None, None), P("row", "col", None, None, None)),
        check_vma=False,
    )
```

```python
import functools
import math

import jax
import jax.numpy as jnp
import numpy as np
from jax import lax
from jax.experimental import pallas as pl
from jax.experimental.pallas import tpu as pltpu
from jax.sharding import PartitionSpec as P

ITERS = 2


ANGLE_STEP = math.pi / 6.0
EPS = 1e-06


def shifted(block, axis, distance):
    devices = range(lax.axis_size(axis))
    route = [((i - distance) % len(devices), i) for i in devices]
    return lax.ppermute(block, axis, route)


def lane_tables(lane_ids):
    lane_index = jnp.arange(lane_ids.shape[-1], dtype=jnp.int32)
    return (lane_index[None, None, :, None] == lane_ids[:, :, None, :]).astype(jnp.float32)


def tile_normals(listing):
    angles = listing[:, 3].astype(jnp.float32) * ANGLE_STEP
    return jnp.stack([jnp.cos(angles), jnp.sin(angles)], axis=1)


def select(block_rows, lane_table):
    return jnp.einsum("xclk,xkm->xclm", block_rows, lane_table, precision=lax.Precision.HIGHEST)


def spread(values, lane_table):
    return jnp.einsum("xclm,xkm->xclk", values, lane_table, precision=lax.Precision.HIGHEST)


def contributions(weighted, normal, tables):
    values = normal[:, :, None, None] * weighted[:, None]
    return (spread(values, tables[:, 0]), spread(values, tables[:, 1]))


def deposit(first_part, second_part, first_ids, second_ids, side_ids, row_begin, row_count):
    pos_first = jnp.where(
        (first_ids >= row_begin) & (first_ids < row_begin + row_count), first_ids, row_count
    )
    pos_second = jnp.where(
        (second_ids >= row_begin) & (second_ids < row_begin + row_count), second_ids, row_count
    )
    buffer = jnp.zeros((row_count, 2) + first_part.shape[1:], jnp.float32)
    buffer = buffer.at[pos_first, 0].add(first_part, mode="drop")
    return buffer.at[pos_second, side_ids].add(-second_part, mode="drop")


def force_squares(values):
    return jnp.sum(values * values, axis=(0, 1, 3))


def image_squares(values):
    return jnp.sum(values * values, axis=(0, 1, 2, 4))


def local(loads, stiffness, tile_info, offsets):
    listing = tile_info[0]
    first_block = listing[:, 0]
    second_block = listing[:, 1]
    upper_flag = listing[:, 2]
    normal = tile_normals(listing)
    tables = lane_tables(offsets[0])
    spring = stiffness[0]
    block_count = loads.shape[1]

    def transpose_apply(disk_field):
        above_rows = shifted(disk_field, "row", -1)
        own_slab, upper_slab = (
            lax.all_gather(disk_field, "col", axis=1, tiled=True),
            lax.all_gather(above_rows, "col", axis=1, tiled=True),
        )
        own_slab = own_slab[0]
        upper_slab = upper_slab[0]
        first_rows = own_slab[first_block]
        second_rows = jnp.where(
            upper_flag[:, None, None, None] == 1, upper_slab[second_block], own_slab[second_block]
        )
        difference = select(first_rows, tables[:, 0]) - select(second_rows, tables[:, 1])
        projected = (
            normal[:, 0, None, None] * difference[:, 0]
            + normal[:, 1, None, None] * difference[:, 1]
        )
        return (spring[:, None, :] * projected)[None]

    def force_total(values):
        return lax.psum(force_squares(values), ("col", "row"))

    residual = loads
    search = transpose_apply(residual)
    forces = jnp.zeros_like(search)
    direction = search
    force_sq = force_total(search)
    for iteration in range(ITERS):
        weighted = spring[:, None, :] * direction[0]
        first_part, second_part = contributions(weighted, normal, tables)
        summed = lax.psum_scatter(
            deposit(
                first_part,
                second_part,
                first_block,
                second_block,
                upper_flag,
                jnp.int32(0),
                block_count * lax.axis_size("col"),
            ),
            "col",
            scatter_dimension=0,
            tiled=True,
        )
        lifted = shifted(summed[:, 1], "row", 1)
        image_field = (summed[:, 0] + lifted)[None]
        image_sq = lax.psum(image_squares(image_field), ("col", "row"))
        step_size = force_sq / (image_sq + EPS)
        forces = forces + step_size[:, None] * direction
        residual = residual - step_size[:, None] * image_field
        if iteration + 1 < ITERS:
            search = transpose_apply(residual)
            force_next = force_total(search)
            direction = search + (force_next / (force_sq + EPS))[:, None] * direction
            force_sq = force_next
    return (forces, residual)


MESH = pl.DeviceIdType.MESH
CORES = 2
SIDE = 2
UNROLL_CHUNKS = 4
INFO_ROW = 8
SPRING_ROW = 12
REPLICATED_LIMIT = 8 * 1024 * 1024
COSINES = [float(v) for v in np.cos(np.arange(6, dtype=np.float32) * np.float32(ANGLE_STEP))]
SINES = [float(v) for v in np.sin(np.arange(6, dtype=np.float32) * np.float32(ANGLE_STEP))]


def gather_kernel(
    line, cols, loads_ref, spring_ref, info_ref, lanes_ref, out_ref, send_sem, recv_sem
):
    col, row = lax.axis_index("col"), lax.axis_index("row")
    z, x = col // SIDE, lax.rem(col, SIDE)
    y, c = row // CORES, lax.rem(row, CORES)
    xa, ya = x + (1 - c) * (1 - 2 * x), y + c * (1 - 2 * y)
    xb, yb = x + c * (1 - 2 * x), y + (1 - c) * (1 - 2 * y)

    def device(zz, xx, yy, cc):
        return {"col": zz * SIDE + xx, "row": yy * CORES + cc}

    def chunk(zz, xx, yy, cc):
        return (yy * CORES + cc) * cols + zz * SIDE + xx

    along = [lax.rem(z + step, line) for step in range(line)]
    partner_a, partner_b = device(z, xa, ya, c), device(z, xb, yb, c)
    partner_core = device(z, x, y, 1 - c)

    barrier = pltpu.get_barrier_semaphore()
    peers = [device(zz, x, y, c) for zz in along[1:]] + [partner_a, partner_b, partner_core]
    for peer in peers:
        pl.semaphore_signal(barrier, inc=1, device_id=peer, device_id_type=MESH)
    me = chunk(z, x, y, c)
    disk_rows, lanes = loads_ref.shape
    tiles, words = info_ref.shape
    out_ref[me, :disk_rows] = loads_ref[...]
    out_ref[me, disk_rows : disk_rows + 2 * tiles] = lanes_ref[...].astype(jnp.float32)
    out_ref[me, disk_rows + INFO_ROW : disk_rows + SPRING_ROW] = jnp.zeros((tiles, lanes), jnp.float32)
    numbers = info_ref[...].astype(jnp.float32)
    listing = jnp.concatenate([numbers[k : k + 1] for k in range(tiles)], axis=1)
    out_ref[me, disk_rows + INFO_ROW : disk_rows + INFO_ROW + 1, : tiles * words] = listing
    out_ref[me, disk_rows + SPRING_ROW : disk_rows + SPRING_ROW + tiles] = spring_ref[...]
    pl.semaphore_wait(barrier, len(peers))

    sent = []

    def send(index, peer):
        copy = pltpu.make_async_remote_copy(
            src_ref=out_ref.at[index],
            dst_ref=out_ref.at[index],
            send_sem=send_sem.at[len(sent)],
            recv_sem=recv_sem.at[index],
            device_id=peer,
            device_id_type=MESH,
        )
        copy.start()
        sent.append(copy)

    def arrive(index):
        pltpu.make_async_remote_copy(
            src_ref=out_ref.at[index],
            dst_ref=out_ref.at[index],
            send_sem=send_sem.at[0],
            recv_sem=recv_sem.at[index],
            device_id=partner_core,
            device_id_type=MESH,
        ).wait_recv()

    for zz in along[1:]:
        send(me, device(zz, x, y, c))
    for peer in (partner_a, partner_b, partner_core):
        send(me, peer)
    order = [along[0]] + [along[s] for s in (1, line - 1)] + [along[s] for s in range(2, line - 1)]
    for position, zz in enumerate(order):
        if position:
            index = chunk(zz, x, y, c)
            arrive(index)
            for peer in (partner_a, partner_b, partner_core):
                send(index, peer)
    for zz in order:
        index = chunk(zz, xa, ya, c)
        arrive(index)
        send(index, partner_b)
        send(index, partner_core)
    for zz in order:
        index = chunk(zz, xb, yb, c)
        arrive(index)
        send(index, partner_core)
    for zz in order:
        index = chunk(zz, 1 - x, 1 - y, c)
        arrive(index)
        send(index, partner_core)
    for xx, yy in ((x, y), (xa, ya), (xb, yb), (1 - x, 1 - y)):
        for zz in order:
            arrive(chunk(zz, xx, yy, 1 - c))
    for copy in sent:
        copy.wait_send()


def solve_kernel(
    dims, place_ref, all_ref, forces_ref, left_ref,
    search_a, search_b, image_a, image_b, rest_ref, info_ref, cos_ref, sin_ref, info_sem,
):
    slabs, blocks, per_blocks, per_tiles, cases, lanes = dims
    chunks = all_ref.shape[0]
    disk_rows = 2 * cases
    cols = chunks // slabs
    base = per_blocks * disk_rows
    listing = pltpu.make_async_copy(
        all_ref.at[:, base + INFO_ROW : base + INFO_ROW + 1, :], info_ref, info_sem
    )
    listing.start()
    for k in range(6):
        cos_ref[k] = COSINES[k]
        sin_ref[k] = SINES[k]
    listing.wait()

    def apply_both(read_block, search_ref, image_ref):
        image_ref[...] = jnp.zeros_like(image_ref)
        sub = lax.broadcasted_iota(jnp.int32, (lanes, lanes), 0)

        def body(step, total):
            parts = []
            for u in range(UNROLL_CHUNKS):
                piece = step * UNROLL_CHUNKS + u
                slab = piece // cols
                for k in range(per_tiles):
                    tile = piece * per_tiles + k
                    info = [info_ref[piece, 0, 4 * k + w].astype(jnp.int32) for w in range(4)]
                    first = slab * blocks + info[0]
                    upper = lax.rem(slab + info[2], slabs)
                    second = upper * blocks + info[1]
                    turn = info[3]
                    n0, n1 = cos_ref[turn], sin_ref[turn]
                    spring = all_ref[piece, base + SPRING_ROW + k : base + SPRING_ROW + k + 1, :]
                    at = base + 2 * k
                    lane_i = all_ref[piece, at : at + 1, :].astype(jnp.int32)
                    lane_j = all_ref[piece, at + 1 : at + 2, :].astype(jnp.int32)
                    vi, vj = read_block(first), read_block(second)
                    pi = n0 * vi[:cases] + n1 * vi[cases:]
                    pj = n0 * vj[:cases] + n1 * vj[cases:]
                    gi = jnp.take_along_axis(
                        pi, jnp.broadcast_to(lane_i, pi.shape), axis=1, mode="promise_in_bounds"
                    )
                    gj = jnp.take_along_axis(
                        pj, jnp.broadcast_to(lane_j, pj.shape), axis=1, mode="promise_in_bounds"
                    )
                    value = spring * (gi - gj)
                    search_ref[tile] = value
                    total = total + value * value
                    weighted = spring * value
                    high = weighted.astype(jnp.bfloat16)
                    rest = weighted - high.astype(jnp.float32)
                    middle = rest.astype(jnp.bfloat16)
                    low = (rest - middle.astype(jnp.float32)).astype(jnp.bfloat16)
                    lhs = jnp.concatenate([high, middle, low], axis=0)
                    hot = jnp.concatenate(
                        [
                            jnp.where(sub == lane_i, 1.0, 0.0).astype(jnp.bfloat16),
                            jnp.where(sub == lane_j, 1.0, 0.0).astype(jnp.bfloat16),
                        ],
                        axis=0,
                    )
                    out = lax.dot_general(
                        lhs, hot, (((1,), (1,)), ((), ())), preferred_element_type=jnp.float32
                    )
                    out = out[:cases] + (out[cases : 2 * cases] + out[2 * cases :])
                    parts.append((first, second, n0, n1, out[:, :lanes], out[:, lanes:]))
            for first, second, n0, n1, one, two in parts:
                image_ref[first, :cases] += n0 * one
                image_ref[first, cases:] += n1 * one
                image_ref[second, :cases] -= n0 * two
                image_ref[second, cases:] -= n1 * two
            return total

        total = lax.fori_loop(
            0, chunks // UNROLL_CHUNKS, body, jnp.zeros((cases, lanes), jnp.float32)
        )
        return jnp.sum(total, axis=1, keepdims=True)

    def chunk_rows(block):
        start = pl.multiple_of(lax.rem(block, per_blocks) * disk_rows, 8)
        return all_ref[block // per_blocks, pl.ds(start, disk_rows), :]

    def squares(field):
        both = jnp.sum(field * field, axis=0)
        return both[:cases] + both[cases:]

    def over_chunks(visit):
        return jnp.sum(
            lax.fori_loop(
                0, chunks, visit, jnp.zeros((cases, lanes), jnp.float32), unroll=2
            ),
            axis=1,
            keepdims=True,
        )

    gamma = apply_both(chunk_rows, search_a, image_a)

    def norm_first(piece, total):
        return total + squares(image_a[pl.ds(piece * per_blocks, per_blocks)])

    alpha = gamma / (over_chunks(norm_first) + EPS)
    alpha_rows = jnp.concatenate([alpha, alpha], axis=0)

    def renew(piece, carry):
        for b in range(per_blocks):
            block = piece * per_blocks + b
            rest_ref[block] = (
                all_ref[piece, b * disk_rows : (b + 1) * disk_rows, :]
                - alpha_rows * image_a[block]
            )
        return carry

    lax.fori_loop(0, chunks, renew, 0, unroll=2)
    gamma_next = apply_both(lambda block: rest_ref[block], search_b, image_b)
    beta = gamma_next / (gamma + EPS)
    beta_rows = jnp.concatenate([beta, beta], axis=0)

    def norm_second(piece, total):
        span = pl.ds(piece * per_blocks, per_blocks)
        return total + squares(image_b[span] + beta_rows * image_a[span])

    alpha_next = gamma_next / (over_chunks(norm_second) + EPS)
    alpha_next_rows = jnp.concatenate([alpha_next, alpha_next], axis=0)
    place = place_ref[0]
    for k in range(per_tiles):
        tile = place * per_tiles + k
        old = search_a[tile]
        forces_ref[0, k] = alpha * old + alpha_next * (search_b[tile] + beta * old)
    for b in range(per_blocks):
        block = place * per_blocks + b
        left = rest_ref[block] - alpha_next_rows * (image_b[block] + beta_rows * image_a[block])
        left_ref[0, b, 0] = left[:cases]
        left_ref[0, b, 1] = left[cases:]


def replicated(cols, rows, loads, stiffness, tile_info, offsets):
    per_blocks, cases, lanes = loads.shape[1], loads.shape[3], loads.shape[4]
    per_tiles = stiffness.shape[1]
    chunks = cols * rows
    height = 2 * per_blocks * cases + SPRING_ROW + per_tiles
    vmem = pl.BlockSpec(memory_space=pltpu.VMEM)
    smem = pl.BlockSpec(memory_space=pltpu.SMEM)
    everything = pl.pallas_call(
        functools.partial(gather_kernel, cols // SIDE, cols),
        out_shape=jax.ShapeDtypeStruct((chunks, height, lanes), jnp.float32),
        in_specs=[vmem] * 4,
        out_specs=vmem,
        scratch_shapes=[
            pltpu.SemaphoreType.DMA((chunks,)),
            pltpu.SemaphoreType.DMA((chunks,)),
        ],
        compiler_params=pltpu.CompilerParams(collective_id=0, has_side_effects=True),
    )(loads.reshape(-1, lanes), stiffness[0], tile_info[0], offsets.reshape(-1, lanes))
    place = (lax.axis_index("row") * cols + lax.axis_index("col")).astype(jnp.int32)
    disk = (chunks * per_blocks, 2 * cases, lanes)
    contact = (chunks * per_tiles, cases, lanes)
    dims = (rows, cols * per_blocks, per_blocks, per_tiles, cases, lanes)
    return pl.pallas_call(
        functools.partial(solve_kernel, dims),
        out_shape=(
            jax.ShapeDtypeStruct((1, per_tiles, cases, lanes), jnp.float32),
            jax.ShapeDtypeStruct(loads.shape, jnp.float32),
        ),
        in_specs=[smem, vmem],
        out_specs=(vmem, vmem),
        scratch_shapes=[
            pltpu.VMEM(contact, jnp.float32),
            pltpu.VMEM(contact, jnp.float32),
            pltpu.VMEM(disk, jnp.float32),
            pltpu.VMEM(disk, jnp.float32),
            pltpu.VMEM(disk, jnp.float32),
            pltpu.SMEM((chunks, 1, lanes), jnp.float32),
            pltpu.SMEM((6,), jnp.float32),
            pltpu.SMEM((6,), jnp.float32),
            pltpu.SemaphoreType.DMA,
        ],
        compiler_params=pltpu.CompilerParams(vmem_limit_bytes=32 * 1024 * 1024),
    )(place[None], everything)


def program_body(cols, rows, loads, stiffness, tile_info, offsets):
    whole = cols * rows * loads.size * 4
    if whole <= REPLICATED_LIMIT and cols % SIDE == 0 and rows == SIDE * CORES and stiffness.shape[1] == 4:
        return replicated(cols, rows, loads, stiffness, tile_info, offsets)
    return local(loads, stiffness, tile_info, offsets)


def solution(mesh):
    placed = (
        P("row", "col", None, None, None),
        P("row", "col", None),
        P("row", "col", None),
        P("row", "col", None, None),
    )
    return jax.shard_map(
        functools.partial(program_body, mesh.shape["col"], mesh.shape["row"]),
        mesh=mesh,
        in_specs=placed,
        out_specs=(P("row", "col", None, None), P("row", "col", None, None, None)),
        check_vma=False,
    )
```

```python
import functools
import math

import jax
import jax.numpy as jnp
import numpy as np
from jax import lax
from jax.experimental import pallas as pl
from jax.experimental.pallas import tpu as pltpu
from jax.sharding import PartitionSpec as P

ITERS = 2


ANGLE_STEP = math.pi / 6.0
EPS = 1e-06


def shifted(block, axis, distance):
    devices = range(lax.axis_size(axis))
    route = [((i - distance) % len(devices), i) for i in devices]
    return lax.ppermute(block, axis, route)


def lane_tables(lane_ids):
    lane_index = jnp.arange(lane_ids.shape[-1], dtype=jnp.int32)
    return (lane_index[None, None, :, None] == lane_ids[:, :, None, :]).astype(jnp.float32)


def tile_normals(listing):
    angles = listing[:, 3].astype(jnp.float32) * ANGLE_STEP
    return jnp.stack([jnp.cos(angles), jnp.sin(angles)], axis=1)


def select(block_rows, lane_table):
    return jnp.einsum("xclk,xkm->xclm", block_rows, lane_table, precision=lax.Precision.HIGHEST)


def spread(values, lane_table):
    return jnp.einsum("xclm,xkm->xclk", values, lane_table, precision=lax.Precision.HIGHEST)


def contributions(weighted, normal, tables):
    values = normal[:, :, None, None] * weighted[:, None]
    return (spread(values, tables[:, 0]), spread(values, tables[:, 1]))


def deposit(first_part, second_part, first_ids, second_ids, side_ids, row_begin, row_count):
    pos_first = jnp.where(
        (first_ids >= row_begin) & (first_ids < row_begin + row_count), first_ids, row_count
    )
    pos_second = jnp.where(
        (second_ids >= row_begin) & (second_ids < row_begin + row_count), second_ids, row_count
    )
    buffer = jnp.zeros((row_count, 2) + first_part.shape[1:], jnp.float32)
    buffer = buffer.at[pos_first, 0].add(first_part, mode="drop")
    return buffer.at[pos_second, side_ids].add(-second_part, mode="drop")


def force_squares(values):
    return jnp.sum(values * values, axis=(0, 1, 3))


def image_squares(values):
    return jnp.sum(values * values, axis=(0, 1, 2, 4))


def local(loads, stiffness, tile_info, offsets):
    listing = tile_info[0]
    first_block = listing[:, 0]
    second_block = listing[:, 1]
    upper_flag = listing[:, 2]
    normal = tile_normals(listing)
    tables = lane_tables(offsets[0])
    spring = stiffness[0]
    block_count = loads.shape[1]

    def transpose_apply(disk_field):
        above_rows = shifted(disk_field, "row", -1)
        own_slab, upper_slab = (
            lax.all_gather(disk_field, "col", axis=1, tiled=True),
            lax.all_gather(above_rows, "col", axis=1, tiled=True),
        )
        own_slab = own_slab[0]
        upper_slab = upper_slab[0]
        first_rows = own_slab[first_block]
        second_rows = jnp.where(
            upper_flag[:, None, None, None] == 1, upper_slab[second_block], own_slab[second_block]
        )
        difference = select(first_rows, tables[:, 0]) - select(second_rows, tables[:, 1])
        projected = (
            normal[:, 0, None, None] * difference[:, 0]
            + normal[:, 1, None, None] * difference[:, 1]
        )
        return (spring[:, None, :] * projected)[None]

    def force_total(values):
        return lax.psum(force_squares(values), ("col", "row"))

    residual = loads
    search = transpose_apply(residual)
    forces = jnp.zeros_like(search)
    direction = search
    force_sq = force_total(search)
    for iteration in range(ITERS):
        weighted = spring[:, None, :] * direction[0]
        first_part, second_part = contributions(weighted, normal, tables)
        summed = lax.psum_scatter(
            deposit(
                first_part,
                second_part,
                first_block,
                second_block,
                upper_flag,
                jnp.int32(0),
                block_count * lax.axis_size("col"),
            ),
            "col",
            scatter_dimension=0,
            tiled=True,
        )
        lifted = shifted(summed[:, 1], "row", 1)
        image_field = (summed[:, 0] + lifted)[None]
        image_sq = lax.psum(image_squares(image_field), ("col", "row"))
        step_size = force_sq / (image_sq + EPS)
        forces = forces + step_size[:, None] * direction
        residual = residual - step_size[:, None] * image_field
        if iteration + 1 < ITERS:
            search = transpose_apply(residual)
            force_next = force_total(search)
            direction = search + (force_next / (force_sq + EPS))[:, None] * direction
            force_sq = force_next
    return (forces, residual)


MESH = pl.DeviceIdType.MESH
CORES = 2
SIDE = 2
UNROLL_CHUNKS = 4
INFO_ROW = 8
SPRING_ROW = 12
REPLICATED_LIMIT = 8 * 1024 * 1024
COSINES = [float(v) for v in np.cos(np.arange(6, dtype=np.float32) * np.float32(ANGLE_STEP))]
SINES = [float(v) for v in np.sin(np.arange(6, dtype=np.float32) * np.float32(ANGLE_STEP))]


def gather_kernel(
    line, cols, loads_ref, spring_ref, info_ref, lanes_ref, out_ref, send_sem, recv_sem
):
    col, row = lax.axis_index("col"), lax.axis_index("row")
    z, x = col // SIDE, lax.rem(col, SIDE)
    y, c = row // CORES, lax.rem(row, CORES)
    xa, ya = x + (1 - c) * (1 - 2 * x), y + c * (1 - 2 * y)
    xb, yb = x + c * (1 - 2 * x), y + (1 - c) * (1 - 2 * y)

    def device(zz, xx, yy, cc):
        return {"col": zz * SIDE + xx, "row": yy * CORES + cc}

    def chunk(zz, xx, yy, cc):
        return (yy * CORES + cc) * cols + zz * SIDE + xx

    along = [lax.rem(z + step, line) for step in range(line)]
    partner_a, partner_b = device(z, xa, ya, c), device(z, xb, yb, c)
    partner_core = device(z, x, y, 1 - c)

    barrier = pltpu.get_barrier_semaphore()
    peers = [device(zz, x, y, c) for zz in along[1:]] + [partner_a, partner_b, partner_core]
    for peer in peers:
        pl.semaphore_signal(barrier, inc=1, device_id=peer, device_id_type=MESH)
    me = chunk(z, x, y, c)
    disk_rows, lanes = loads_ref.shape
    tiles, words = info_ref.shape
    out_ref[me, :disk_rows] = loads_ref[...]
    out_ref[me, disk_rows : disk_rows + 2 * tiles] = lanes_ref[...].astype(jnp.float32)
    out_ref[me, disk_rows + INFO_ROW : disk_rows + SPRING_ROW] = jnp.zeros((tiles, lanes), jnp.float32)
    numbers = info_ref[...].astype(jnp.float32)
    listing = jnp.concatenate([numbers[k : k + 1] for k in range(tiles)], axis=1)
    out_ref[me, disk_rows + INFO_ROW : disk_rows + INFO_ROW + 1, : tiles * words] = listing
    out_ref[me, disk_rows + SPRING_ROW : disk_rows + SPRING_ROW + tiles] = spring_ref[...]
    pl.semaphore_wait(barrier, len(peers))

    sent = []

    def send(index, peer):
        copy = pltpu.make_async_remote_copy(
            src_ref=out_ref.at[index],
            dst_ref=out_ref.at[index],
            send_sem=send_sem.at[len(sent)],
            recv_sem=recv_sem.at[index],
            device_id=peer,
            device_id_type=MESH,
        )
        copy.start()
        sent.append(copy)

    def arrive(index):
        pltpu.make_async_remote_copy(
            src_ref=out_ref.at[index],
            dst_ref=out_ref.at[index],
            send_sem=send_sem.at[0],
            recv_sem=recv_sem.at[index],
            device_id=partner_core,
            device_id_type=MESH,
        ).wait_recv()

    for zz in along[1:]:
        send(me, device(zz, x, y, c))
    for peer in (partner_a, partner_b, partner_core):
        send(me, peer)
    order = [along[0]] + [along[s] for s in (1, line - 1)] + [along[s] for s in range(2, line - 1)]
    for position, zz in enumerate(order):
        if position:
            index = chunk(zz, x, y, c)
            arrive(index)
            for peer in (partner_a, partner_b, partner_core):
                send(index, peer)
    for zz in order:
        index = chunk(zz, xa, ya, c)
        arrive(index)
        send(index, partner_b)
        send(index, partner_core)
    for zz in order:
        index = chunk(zz, xb, yb, c)
        arrive(index)
        send(index, partner_core)
    for zz in order:
        index = chunk(zz, 1 - x, 1 - y, c)
        arrive(index)
        send(index, partner_core)
    for xx, yy in ((x, y), (xa, ya), (xb, yb), (1 - x, 1 - y)):
        for zz in order:
            arrive(chunk(zz, xx, yy, 1 - c))
    for copy in sent:
        copy.wait_send()


def solve_kernel(
    dims, place_ref, all_ref, forces_ref, left_ref,
    search_a, search_b, image_a, image_b, rest_ref,
    index_vmem, normal_vmem, index_ref, normal_ref, table_sem,
):
    slabs, blocks, per_blocks, per_tiles, cases, lanes = dims
    chunks = all_ref.shape[0]
    disk_rows = 2 * cases
    cols = chunks // slabs
    base = per_blocks * disk_rows

    words = all_ref[:, base + INFO_ROW, :].astype(jnp.int32)
    after = pltpu.roll(words, lanes - 1, 1)
    word = lax.broadcasted_iota(jnp.int32, words.shape, 1) & 3
    piece_of = lax.broadcasted_iota(jnp.int32, words.shape, 0)
    slab_of = jnp.zeros_like(words)
    for s in range(1, slabs):
        slab_of = slab_of + (piece_of >= s * cols).astype(jnp.int32)
    upper_of = slab_of + after
    upper_of = jnp.where(upper_of >= slabs, upper_of - slabs, upper_of)
    index_vmem[...] = jnp.where(word == 0, slab_of, upper_of) * blocks + words
    turn = jnp.where(word == 2, after, words)
    normals = jnp.zeros(words.shape, jnp.float32)
    for k in range(6):
        normals = jnp.where(turn == k, jnp.where(word == 2, COSINES[k], SINES[k]), normals)
    normal_vmem[...] = normals
    image_a[...] = jnp.zeros_like(image_a)
    image_b[...] = jnp.zeros_like(image_b)
    tables = [
        pltpu.make_async_copy(index_vmem, index_ref, table_sem.at[0]),
        pltpu.make_async_copy(normal_vmem, normal_ref, table_sem.at[1]),
    ]
    for table in tables:
        table.start()

    def unpack(piece, carry):
        for b in range(per_blocks):
            rest_ref[piece * per_blocks + b] = all_ref[piece, b * disk_rows : (b + 1) * disk_rows, :]
        return carry

    lax.fori_loop(0, chunks, unpack, 0, unroll=4)
    for table in tables:
        table.wait()

    def apply_both(search_ref, image_ref):
        sub = lax.broadcasted_iota(jnp.int32, (lanes, lanes), 0)

        def body(step, total):
            parts = []
            for u in range(UNROLL_CHUNKS):
                piece = step * UNROLL_CHUNKS + u
                for k in range(per_tiles):
                    tile = piece * per_tiles + k
                    first, second = index_ref[piece, 4 * k], index_ref[piece, 4 * k + 1]
                    n0, n1 = normal_ref[piece, 4 * k + 2], normal_ref[piece, 4 * k + 3]
                    at = base + SPRING_ROW + k
                    spring = all_ref[piece, at : at + 1, :]
                    at = base + 2 * k
                    lane_i = all_ref[piece, at : at + 1, :].astype(jnp.int32)
                    lane_j = all_ref[piece, at + 1 : at + 2, :].astype(jnp.int32)
                    vi, vj = rest_ref[first], rest_ref[second]
                    pi = n0 * vi[:cases] + n1 * vi[cases:]
                    pj = n0 * vj[:cases] + n1 * vj[cases:]
                    gi = jnp.take_along_axis(
                        pi, jnp.broadcast_to(lane_i, pi.shape), axis=1, mode="promise_in_bounds"
                    )
                    gj = jnp.take_along_axis(
                        pj, jnp.broadcast_to(lane_j, pj.shape), axis=1, mode="promise_in_bounds"
                    )
                    value = spring * (gi - gj)
                    search_ref[tile] = value
                    total = total + value * value
                    weighted = spring * value
                    high = weighted.astype(jnp.bfloat16)
                    rest = weighted - high.astype(jnp.float32)
                    middle = rest.astype(jnp.bfloat16)
                    low = (rest - middle.astype(jnp.float32)).astype(jnp.bfloat16)
                    lhs = jnp.concatenate([high, middle, low], axis=0)
                    hot = jnp.concatenate(
                        [
                            jnp.where(sub == lane_i, 1.0, 0.0).astype(jnp.bfloat16),
                            jnp.where(sub == lane_j, 1.0, 0.0).astype(jnp.bfloat16),
                        ],
                        axis=0,
                    )
                    out = lax.dot_general(
                        lhs, hot, (((1,), (1,)), ((), ())), preferred_element_type=jnp.float32
                    )
                    out = out[:cases] + (out[cases : 2 * cases] + out[2 * cases :])
                    parts.append((first, second, n0, n1, out[:, :lanes], out[:, lanes:]))
            for first, second, n0, n1, one, two in parts:
                image_ref[first, :cases] += n0 * one
                image_ref[first, cases:] += n1 * one
                image_ref[second, :cases] -= n0 * two
                image_ref[second, cases:] -= n1 * two
            return total

        total = lax.fori_loop(
            0, chunks // UNROLL_CHUNKS, body, jnp.zeros((cases, lanes), jnp.float32)
        )
        return jnp.sum(total, axis=1, keepdims=True)

    def squares(field):
        both = jnp.sum(field * field, axis=0)
        return both[:cases] + both[cases:]

    def over_chunks(visit):
        return jnp.sum(
            lax.fori_loop(
                0, chunks, visit, jnp.zeros((cases, lanes), jnp.float32), unroll=2
            ),
            axis=1,
            keepdims=True,
        )

    gamma = apply_both(search_a, image_a)

    def norm_first(piece, total):
        return total + squares(image_a[pl.ds(piece * per_blocks, per_blocks)])

    alpha = gamma / (over_chunks(norm_first) + EPS)
    alpha_rows = jnp.concatenate([alpha, alpha], axis=0)

    def renew(piece, carry):
        for b in range(per_blocks):
            block = piece * per_blocks + b
            rest_ref[block] = rest_ref[block] - alpha_rows * image_a[block]
        return carry

    lax.fori_loop(0, chunks, renew, 0, unroll=2)
    gamma_next = apply_both(search_b, image_b)
    beta = gamma_next / (gamma + EPS)
    beta_rows = jnp.concatenate([beta, beta], axis=0)

    def norm_second(piece, total):
        span = pl.ds(piece * per_blocks, per_blocks)
        return total + squares(image_b[span] + beta_rows * image_a[span])

    alpha_next = gamma_next / (over_chunks(norm_second) + EPS)
    alpha_next_rows = jnp.concatenate([alpha_next, alpha_next], axis=0)
    place = place_ref[0]
    for k in range(per_tiles):
        tile = place * per_tiles + k
        old = search_a[tile]
        forces_ref[0, k] = alpha * old + alpha_next * (search_b[tile] + beta * old)
    for b in range(per_blocks):
        block = place * per_blocks + b
        left = rest_ref[block] - alpha_next_rows * (image_b[block] + beta_rows * image_a[block])
        left_ref[0, b, 0] = left[:cases]
        left_ref[0, b, 1] = left[cases:]


def replicated(cols, rows, loads, stiffness, tile_info, offsets):
    per_blocks, cases, lanes = loads.shape[1], loads.shape[3], loads.shape[4]
    per_tiles = stiffness.shape[1]
    chunks = cols * rows
    height = 2 * per_blocks * cases + SPRING_ROW + per_tiles
    vmem = pl.BlockSpec(memory_space=pltpu.VMEM)
    smem = pl.BlockSpec(memory_space=pltpu.SMEM)
    everything = pl.pallas_call(
        functools.partial(gather_kernel, cols // SIDE, cols),
        out_shape=pltpu.VMEM((chunks, height, lanes), jnp.float32),
        in_specs=[vmem] * 4,
        out_specs=vmem,
        scratch_shapes=[
            pltpu.SemaphoreType.DMA((chunks,)),
            pltpu.SemaphoreType.DMA((chunks,)),
        ],
        compiler_params=pltpu.CompilerParams(collective_id=0, has_side_effects=True),
    )(loads.reshape(-1, lanes), stiffness[0], tile_info[0], offsets.reshape(-1, lanes))
    place = (lax.axis_index("row") * cols + lax.axis_index("col")).astype(jnp.int32)
    disk = (chunks * per_blocks, 2 * cases, lanes)
    contact = (chunks * per_tiles, cases, lanes)
    dims = (rows, cols * per_blocks, per_blocks, per_tiles, cases, lanes)
    return pl.pallas_call(
        functools.partial(solve_kernel, dims),
        out_shape=(
            jax.ShapeDtypeStruct((1, per_tiles, cases, lanes), jnp.float32),
            jax.ShapeDtypeStruct(loads.shape, jnp.float32),
        ),
        in_specs=[smem, vmem],
        out_specs=(vmem, vmem),
        scratch_shapes=[
            pltpu.VMEM(contact, jnp.float32),
            pltpu.VMEM(contact, jnp.float32),
            pltpu.VMEM(disk, jnp.float32),
            pltpu.VMEM(disk, jnp.float32),
            pltpu.VMEM(disk, jnp.float32),
            pltpu.VMEM((chunks, lanes), jnp.int32),
            pltpu.VMEM((chunks, lanes), jnp.float32),
            pltpu.SMEM((chunks, lanes), jnp.int32),
            pltpu.SMEM((chunks, lanes), jnp.float32),
            pltpu.SemaphoreType.DMA((2,)),
        ],
        compiler_params=pltpu.CompilerParams(vmem_limit_bytes=32 * 1024 * 1024),
    )(
        place[None], pltpu.with_memory_space_constraint(everything, pltpu.VMEM)
    )


def program_body(cols, rows, loads, stiffness, tile_info, offsets):
    whole = cols * rows * loads.size * 4
    if whole <= REPLICATED_LIMIT and cols % SIDE == 0 and rows == SIDE * CORES and stiffness.shape[1] == 4:
        return replicated(cols, rows, loads, stiffness, tile_info, offsets)
    return local(loads, stiffness, tile_info, offsets)


def solution(mesh):
    placed = (
        P("row", "col", None, None, None),
        P("row", "col", None),
        P("row", "col", None),
        P("row", "col", None, None),
    )
    return jax.shard_map(
        functools.partial(program_body, mesh.shape["col"], mesh.shape["row"]),
        mesh=mesh,
        in_specs=placed,
        out_specs=(P("row", "col", None, None), P("row", "col", None, None, None)),
        check_vma=False,
    )
```

```python
import functools
import math

import jax
import jax.numpy as jnp
import numpy as np
from jax import lax
from jax.experimental import pallas as pl
from jax.experimental.pallas import tpu as pltpu
from jax.sharding import PartitionSpec as P

ITERS = 2


ANGLE_STEP = math.pi / 6.0
EPS = 1e-06


def shifted(block, axis, distance):
    devices = range(lax.axis_size(axis))
    route = [((i - distance) % len(devices), i) for i in devices]
    return lax.ppermute(block, axis, route)


def lane_tables(lane_ids):
    lane_index = jnp.arange(lane_ids.shape[-1], dtype=jnp.int32)
    return (lane_index[None, None, :, None] == lane_ids[:, :, None, :]).astype(jnp.float32)


def tile_normals(listing):
    angles = listing[:, 3].astype(jnp.float32) * ANGLE_STEP
    return jnp.stack([jnp.cos(angles), jnp.sin(angles)], axis=1)


def select(block_rows, lane_table):
    return jnp.einsum("xclk,xkm->xclm", block_rows, lane_table, precision=lax.Precision.HIGHEST)


def spread(values, lane_table):
    return jnp.einsum("xclm,xkm->xclk", values, lane_table, precision=lax.Precision.HIGHEST)


def contributions(weighted, normal, tables):
    values = normal[:, :, None, None] * weighted[:, None]
    return (spread(values, tables[:, 0]), spread(values, tables[:, 1]))


def deposit(first_part, second_part, first_ids, second_ids, side_ids, row_begin, row_count):
    pos_first = jnp.where(
        (first_ids >= row_begin) & (first_ids < row_begin + row_count), first_ids, row_count
    )
    pos_second = jnp.where(
        (second_ids >= row_begin) & (second_ids < row_begin + row_count), second_ids, row_count
    )
    buffer = jnp.zeros((row_count, 2) + first_part.shape[1:], jnp.float32)
    buffer = buffer.at[pos_first, 0].add(first_part, mode="drop")
    return buffer.at[pos_second, side_ids].add(-second_part, mode="drop")


def force_squares(values):
    return jnp.sum(values * values, axis=(0, 1, 3))


def image_squares(values):
    return jnp.sum(values * values, axis=(0, 1, 2, 4))


def local(loads, stiffness, tile_info, offsets):
    listing = tile_info[0]
    first_block = listing[:, 0]
    second_block = listing[:, 1]
    upper_flag = listing[:, 2]
    normal = tile_normals(listing)
    tables = lane_tables(offsets[0])
    spring = stiffness[0]
    block_count = loads.shape[1]

    def transpose_apply(disk_field):
        above_rows = shifted(disk_field, "row", -1)
        own_slab, upper_slab = (
            lax.all_gather(disk_field, "col", axis=1, tiled=True),
            lax.all_gather(above_rows, "col", axis=1, tiled=True),
        )
        own_slab = own_slab[0]
        upper_slab = upper_slab[0]
        first_rows = own_slab[first_block]
        second_rows = jnp.where(
            upper_flag[:, None, None, None] == 1, upper_slab[second_block], own_slab[second_block]
        )
        difference = select(first_rows, tables[:, 0]) - select(second_rows, tables[:, 1])
        projected = (
            normal[:, 0, None, None] * difference[:, 0]
            + normal[:, 1, None, None] * difference[:, 1]
        )
        return (spring[:, None, :] * projected)[None]

    def force_total(values):
        return lax.psum(force_squares(values), ("col", "row"))

    residual = loads
    search = transpose_apply(residual)
    forces = jnp.zeros_like(search)
    direction = search
    force_sq = force_total(search)
    for iteration in range(ITERS):
        weighted = spring[:, None, :] * direction[0]
        first_part, second_part = contributions(weighted, normal, tables)
        summed = lax.psum_scatter(
            deposit(
                first_part,
                second_part,
                first_block,
                second_block,
                upper_flag,
                jnp.int32(0),
                block_count * lax.axis_size("col"),
            ),
            "col",
            scatter_dimension=0,
            tiled=True,
        )
        lifted = shifted(summed[:, 1], "row", 1)
        image_field = (summed[:, 0] + lifted)[None]
        image_sq = lax.psum(image_squares(image_field), ("col", "row"))
        step_size = force_sq / (image_sq + EPS)
        forces = forces + step_size[:, None] * direction
        residual = residual - step_size[:, None] * image_field
        if iteration + 1 < ITERS:
            search = transpose_apply(residual)
            force_next = force_total(search)
            direction = search + (force_next / (force_sq + EPS))[:, None] * direction
            force_sq = force_next
    return (forces, residual)


MESH = pl.DeviceIdType.MESH
CORES = 2
SIDE = 2
UNROLL_CHUNKS = 4
INFO_ROW = 8
SPRING_ROW = 12
REPLICATED_LIMIT = 8 * 1024 * 1024
COSINES = [float(v) for v in np.cos(np.arange(6, dtype=np.float32) * np.float32(ANGLE_STEP))]
SINES = [float(v) for v in np.sin(np.arange(6, dtype=np.float32) * np.float32(ANGLE_STEP))]


def gather_kernel(
    line, cols, loads_ref, spring_ref, info_ref, lanes_ref, out_ref, send_sem, recv_sem
):
    col, row = lax.axis_index("col"), lax.axis_index("row")
    z, x = col // SIDE, lax.rem(col, SIDE)
    y, c = row // CORES, lax.rem(row, CORES)
    xa, ya = x + (1 - c) * (1 - 2 * x), y + c * (1 - 2 * y)
    xb, yb = x + c * (1 - 2 * x), y + (1 - c) * (1 - 2 * y)

    def device(zz, xx, yy, cc):
        return {"col": zz * SIDE + xx, "row": yy * CORES + cc}

    def chunk(zz, xx, yy, cc):
        return (yy * CORES + cc) * cols + zz * SIDE + xx

    along = [lax.rem(z + step, line) for step in range(line)]
    partner_a, partner_b = device(z, xa, ya, c), device(z, xb, yb, c)
    partner_core = device(z, x, y, 1 - c)

    barrier = pltpu.get_barrier_semaphore()
    peers = [device(zz, x, y, c) for zz in along[1:]] + [partner_a, partner_b, partner_core]
    for peer in peers:
        pl.semaphore_signal(barrier, inc=1, device_id=peer, device_id_type=MESH)
    me = chunk(z, x, y, c)
    disk_rows, lanes = loads_ref.shape
    tiles, words = info_ref.shape
    out_ref[me, :disk_rows] = loads_ref[...]
    out_ref[me, disk_rows : disk_rows + 2 * tiles] = lanes_ref[...].astype(jnp.float32)
    out_ref[me, disk_rows + INFO_ROW : disk_rows + SPRING_ROW] = jnp.zeros((tiles, lanes), jnp.float32)
    numbers = info_ref[...].astype(jnp.float32)
    listing = jnp.concatenate([numbers[k : k + 1] for k in range(tiles)], axis=1)
    out_ref[me, disk_rows + INFO_ROW : disk_rows + INFO_ROW + 1, : tiles * words] = listing
    out_ref[me, disk_rows + SPRING_ROW : disk_rows + SPRING_ROW + tiles] = spring_ref[...]
    pl.semaphore_wait(barrier, len(peers))

    sent = []

    def send(index, peer):
        copy = pltpu.make_async_remote_copy(
            src_ref=out_ref.at[index],
            dst_ref=out_ref.at[index],
            send_sem=send_sem.at[len(sent)],
            recv_sem=recv_sem.at[index],
            device_id=peer,
            device_id_type=MESH,
        )
        copy.start()
        sent.append(copy)

    def arrive(index):
        pltpu.make_async_remote_copy(
            src_ref=out_ref.at[index],
            dst_ref=out_ref.at[index],
            send_sem=send_sem.at[0],
            recv_sem=recv_sem.at[index],
            device_id=partner_core,
            device_id_type=MESH,
        ).wait_recv()

    for zz in along[1:]:
        send(me, device(zz, x, y, c))
    for peer in (partner_a, partner_b, partner_core):
        send(me, peer)
    order = [along[0]] + [along[s] for s in (1, line - 1)] + [along[s] for s in range(2, line - 1)]
    for position, zz in enumerate(order):
        if position:
            index = chunk(zz, x, y, c)
            arrive(index)
            for peer in (partner_a, partner_b, partner_core):
                send(index, peer)
    for zz in order:
        index = chunk(zz, xa, ya, c)
        arrive(index)
        send(index, partner_b)
        send(index, partner_core)
    for zz in order:
        index = chunk(zz, xb, yb, c)
        arrive(index)
        send(index, partner_core)
    for zz in order:
        index = chunk(zz, 1 - x, 1 - y, c)
        arrive(index)
        send(index, partner_core)
    for xx, yy in ((x, y), (xa, ya), (xb, yb), (1 - x, 1 - y)):
        for zz in order:
            arrive(chunk(zz, xx, yy, 1 - c))
    for copy in sent:
        copy.wait_send()


def solve_kernel(
    dims, place_ref, all_ref, forces_ref, left_ref,
    search_a, search_b, image_a, image_b, rest_ref,
    pieces_ref, held_ref, index_vmem, normal_vmem, index_ref, normal_ref, table_sem,
):
    slabs, blocks, per_blocks, per_tiles, cases, lanes = dims
    chunks = all_ref.shape[0]
    disk_rows = 2 * cases
    cols = chunks // slabs
    base = per_blocks * disk_rows

    words = all_ref[:, base + INFO_ROW, :].astype(jnp.int32)
    after = pltpu.roll(words, lanes - 1, 1)
    word = lax.broadcasted_iota(jnp.int32, words.shape, 1) & 3
    piece_of = lax.broadcasted_iota(jnp.int32, words.shape, 0)
    slab_of = jnp.zeros_like(words)
    for s in range(1, slabs):
        slab_of = slab_of + (piece_of >= s * cols).astype(jnp.int32)
    upper_of = slab_of + after
    upper_of = jnp.where(upper_of >= slabs, upper_of - slabs, upper_of)
    index_vmem[...] = jnp.where(word == 0, slab_of, upper_of) * blocks + words
    turn = jnp.where(word == 2, after, words)
    normals = jnp.zeros(words.shape, jnp.float32)
    for k in range(6):
        normals = jnp.where(turn == k, jnp.where(word == 2, COSINES[k], SINES[k]), normals)
    normal_vmem[...] = normals
    image_a[...] = jnp.zeros_like(image_a)
    image_b[...] = jnp.zeros_like(image_b)
    tables = [
        pltpu.make_async_copy(index_vmem, index_ref, table_sem.at[0]),
        pltpu.make_async_copy(normal_vmem, normal_ref, table_sem.at[1]),
    ]
    for table in tables:
        table.start()

    def unpack(piece, carry):
        for b in range(per_blocks):
            rest_ref[piece * per_blocks + b] = all_ref[piece, b * disk_rows : (b + 1) * disk_rows, :]
        return carry

    lax.fori_loop(0, chunks, unpack, 0, unroll=4)
    for table in tables:
        table.wait()

    def apply_both(search_ref, image_ref):
        sub = lax.broadcasted_iota(jnp.int32, (lanes, lanes), 0).astype(jnp.float32).astype(jnp.bfloat16)
        one, zero = jnp.bfloat16(1), jnp.bfloat16(0)

        step_tiles = UNROLL_CHUNKS * per_tiles
        held_ref[...] = jnp.zeros_like(held_ref)

        def deposit_step(step):
            for t in range(step_tiles):
                piece, k = step * UNROLL_CHUNKS + t // per_tiles, t % per_tiles
                first, second = index_ref[piece, 4 * k], index_ref[piece, 4 * k + 1]
                n0, n1 = normal_ref[piece, 4 * k + 2], normal_ref[piece, 4 * k + 3]
                one_end, other_end = held_ref[t, :, :lanes], held_ref[t, :, lanes:]
                image_ref[first, :cases] += n0 * one_end
                image_ref[first, cases:] += n1 * one_end
                image_ref[second, :cases] -= n0 * other_end
                image_ref[second, cases:] -= n1 * other_end

        def prepare(step, total):
            for t in range(step_tiles):
                piece, k = step * UNROLL_CHUNKS + t // per_tiles, t % per_tiles
                first, second = index_ref[piece, 4 * k], index_ref[piece, 4 * k + 1]
                n0, n1 = normal_ref[piece, 4 * k + 2], normal_ref[piece, 4 * k + 3]
                at = base + SPRING_ROW + k
                spring = all_ref[piece, at : at + 1, :]
                at = base + 2 * k
                lane_i = all_ref[piece, at : at + 1, :].astype(jnp.int32)
                lane_j = all_ref[piece, at + 1 : at + 2, :].astype(jnp.int32)
                vi, vj = rest_ref[first], rest_ref[second]
                pi = n0 * vi[:cases] + n1 * vi[cases:]
                pj = n0 * vj[:cases] + n1 * vj[cases:]
                gi = jnp.take_along_axis(
                    pi, jnp.broadcast_to(lane_i, pi.shape), axis=1, mode="promise_in_bounds"
                )
                gj = jnp.take_along_axis(
                    pj, jnp.broadcast_to(lane_j, pj.shape), axis=1, mode="promise_in_bounds"
                )
                value = spring * (gi - gj)
                search_ref[piece * per_tiles + k] = value
                total = total + value * value
                weighted = spring * value
                high = weighted.astype(jnp.bfloat16)
                rest = weighted - high.astype(jnp.float32)
                middle = rest.astype(jnp.bfloat16)
                low = (rest - middle.astype(jnp.float32)).astype(jnp.bfloat16)
                pieces_ref[t] = jnp.concatenate([high, middle, low], axis=0)
            return total

        def products(step):
            for t in range(step_tiles):
                piece, k = step * UNROLL_CHUNKS + t // per_tiles, t % per_tiles
                at = base + 2 * k
                spot_i = all_ref[piece, at : at + 1, :].astype(jnp.bfloat16)
                spot_j = all_ref[piece, at + 1 : at + 2, :].astype(jnp.bfloat16)
                hot = jnp.concatenate(
                    [jnp.where(sub == spot_i, one, zero), jnp.where(sub == spot_j, one, zero)],
                    axis=0,
                )
                out = lax.dot_general(
                    pieces_ref[t], hot, (((1,), (1,)), ((), ())), preferred_element_type=jnp.float32
                )
                held_ref[t] = out[:cases] + (out[cases : 2 * cases] + out[2 * cases :])

        def body(step, total):
            deposit_step(jnp.maximum(step - 1, 0))
            products(step)
            return prepare(step + 1, total)

        steps = chunks // UNROLL_CHUNKS
        total = prepare(0, jnp.zeros((cases, lanes), jnp.float32))
        total = lax.fori_loop(0, steps - 1, body, total)
        deposit_step(steps - 2)
        products(steps - 1)
        deposit_step(steps - 1)
        return jnp.sum(total, axis=1, keepdims=True)

    def squares(field):
        both = jnp.sum(field * field, axis=0)
        return both[:cases] + both[cases:]

    def over_chunks(visit):
        return jnp.sum(
            lax.fori_loop(
                0, chunks, visit, jnp.zeros((cases, lanes), jnp.float32), unroll=2
            ),
            axis=1,
            keepdims=True,
        )

    gamma = apply_both(search_a, image_a)

    def norm_first(piece, total):
        return total + squares(image_a[pl.ds(piece * per_blocks, per_blocks)])

    alpha = gamma / (over_chunks(norm_first) + EPS)
    alpha_rows = jnp.concatenate([alpha, alpha], axis=0)

    def renew(piece, carry):
        for b in range(per_blocks):
            block = piece * per_blocks + b
            rest_ref[block] = rest_ref[block] - alpha_rows * image_a[block]
        return carry

    lax.fori_loop(0, chunks, renew, 0, unroll=2)
    gamma_next = apply_both(search_b, image_b)
    beta = gamma_next / (gamma + EPS)
    beta_rows = jnp.concatenate([beta, beta], axis=0)

    def norm_second(piece, total):
        span = pl.ds(piece * per_blocks, per_blocks)
        return total + squares(image_b[span] + beta_rows * image_a[span])

    alpha_next = gamma_next / (over_chunks(norm_second) + EPS)
    alpha_next_rows = jnp.concatenate([alpha_next, alpha_next], axis=0)
    place = place_ref[0]
    for k in range(per_tiles):
        tile = place * per_tiles + k
        old = search_a[tile]
        forces_ref[0, k] = alpha * old + alpha_next * (search_b[tile] + beta * old)
    for b in range(per_blocks):
        block = place * per_blocks + b
        left = rest_ref[block] - alpha_next_rows * (image_b[block] + beta_rows * image_a[block])
        left_ref[0, b, 0] = left[:cases]
        left_ref[0, b, 1] = left[cases:]


def replicated(cols, rows, loads, stiffness, tile_info, offsets):
    per_blocks, cases, lanes = loads.shape[1], loads.shape[3], loads.shape[4]
    per_tiles = stiffness.shape[1]
    chunks = cols * rows
    height = 2 * per_blocks * cases + SPRING_ROW + per_tiles
    vmem = pl.BlockSpec(memory_space=pltpu.VMEM)
    smem = pl.BlockSpec(memory_space=pltpu.SMEM)
    everything = pl.pallas_call(
        functools.partial(gather_kernel, cols // SIDE, cols),
        out_shape=pltpu.VMEM((chunks, height, lanes), jnp.float32),
        in_specs=[vmem] * 4,
        out_specs=vmem,
        scratch_shapes=[
            pltpu.SemaphoreType.DMA((chunks,)),
            pltpu.SemaphoreType.DMA((chunks,)),
        ],
        compiler_params=pltpu.CompilerParams(collective_id=0, has_side_effects=True),
    )(loads.reshape(-1, lanes), stiffness[0], tile_info[0], offsets.reshape(-1, lanes))
    place = (lax.axis_index("row") * cols + lax.axis_index("col")).astype(jnp.int32)
    disk = (chunks * per_blocks, 2 * cases, lanes)
    contact = (chunks * per_tiles, cases, lanes)
    dims = (rows, cols * per_blocks, per_blocks, per_tiles, cases, lanes)
    return pl.pallas_call(
        functools.partial(solve_kernel, dims),
        out_shape=(
            jax.ShapeDtypeStruct((1, per_tiles, cases, lanes), jnp.float32),
            jax.ShapeDtypeStruct(loads.shape, jnp.float32),
        ),
        in_specs=[smem, vmem],
        out_specs=(vmem, vmem),
        scratch_shapes=[
            pltpu.VMEM(contact, jnp.float32),
            pltpu.VMEM(contact, jnp.float32),
            pltpu.VMEM(disk, jnp.float32),
            pltpu.VMEM(disk, jnp.float32),
            pltpu.VMEM(disk, jnp.float32),
            pltpu.VMEM((UNROLL_CHUNKS * per_tiles, 3 * cases, lanes), jnp.bfloat16),
            pltpu.VMEM((UNROLL_CHUNKS * per_tiles, cases, 2 * lanes), jnp.float32),
            pltpu.VMEM((chunks, lanes), jnp.int32),
            pltpu.VMEM((chunks, lanes), jnp.float32),
            pltpu.SMEM((chunks, lanes), jnp.int32),
            pltpu.SMEM((chunks, lanes), jnp.float32),
            pltpu.SemaphoreType.DMA((2,)),
        ],
        compiler_params=pltpu.CompilerParams(vmem_limit_bytes=32 * 1024 * 1024),
    )(
        place[None], pltpu.with_memory_space_constraint(everything, pltpu.VMEM)
    )


def program_body(cols, rows, loads, stiffness, tile_info, offsets):
    whole = cols * rows * loads.size * 4
    if whole <= REPLICATED_LIMIT and cols % SIDE == 0 and rows == SIDE * CORES and stiffness.shape[1] == 4:
        return replicated(cols, rows, loads, stiffness, tile_info, offsets)
    return local(loads, stiffness, tile_info, offsets)


def solution(mesh):
    placed = (
        P("row", "col", None, None, None),
        P("row", "col", None),
        P("row", "col", None),
        P("row", "col", None, None),
    )
    return jax.shard_map(
        functools.partial(program_body, mesh.shape["col"], mesh.shape["row"]),
        mesh=mesh,
        in_specs=placed,
        out_specs=(P("row", "col", None, None), P("row", "col", None, None, None)),
        check_vma=False,
    )
```
